32 devices in a mesh: gx: 4 (over x, core), gy: 4 (over z), gz: 2 (over y).
Axes of the slice: x: 2, y: 2, z: 4, core: 2. Of those that a mesh axis runs over, the one named last changes fastest.
Arguments:
- displacement: float32 [3, 32, 32, 256], P(None, 'gx', 'gy', 'gz'), may hold values from -0.25 to 0.25
- bond_intact: int32 [61, 32, 32, 256], P(None, 'gx', 'gy', 'gz'), may hold values 0 or 1
Outputs:
- force: float32 [3, 32, 32, 256], P(None, 'gx', 'gy', 'gz')
- dilatation: float32 [32, 32, 256], P('gx', 'gy', 'gz')
The draws below stay inside these ranges and needn't reach their ends.
All inputs are finite; a program needn't handle non-finite values. No bound on the sum of `bond_intact` on one device may be relied on, other than what follows from the above.
Results may differ from the reference program's by a relative error of at most 0.000063.
Values sent between devices are 32-bit elements; how exact they have to be, the bound alone decides.
A program may use at most 128 MiB of HBM per device.

```python
import math
import jax
import jax.numpy as jnp
from jax import lax

HALF_BONDS = 61
NX = 32
NY = 32
NZ = 256


def set_ends(result, own_key, least, high):
    index_at = [jax.random.randint(jax.random.fold_in(own_key, axis), (), 0, length) for axis, length in enumerate(result.shape)]
    widest = result.shape.index(max(result.shape))
    beside = index_at[:widest] + [(index_at[widest] + 1) % result.shape[widest]] + index_at[widest + 1:]
    return result.at[tuple(index_at)].set(least).at[tuple(beside)].set(high)


def shard_levels(key, shape, split, low, high):
    factor_of, own = 1.0, jax.random.fold_in(key, 6)
    for position, parts in split:
        heights = jnp.exp(jax.random.uniform(jax.random.fold_in(own, position), (parts,), jnp.float32, low / len(split), high / len(split)))
        factor_of = factor_of * jnp.repeat(heights, shape[position] // parts).reshape([-1 if axis == position else 1 for axis in range(len(shape))])
    return factor_of


def bell_draw(key, dims, scale, most, cuts=(), dtype=jnp.bfloat16):
    entries = scale * jax.random.normal(key, dims, jnp.float32)
    if cuts:
        entries = entries * shard_levels(key, dims, cuts, -0.22, 0.18)
    return jnp.clip(entries, -most, most).astype(dtype)


def setup_inputs(seed: int = 0) -> dict:
    key_list = jax.random.split(jax.random.key(seed), 3)
    displacement = bell_draw(key_list[0], (3, NX, NY, NZ), 0.05, 0.25, ((1, 4), (2, 4), (3, 2)), jnp.float32)
    bond_intact = set_ends((jax.random.randint(key_list[1], (HALF_BONDS, NX, NY, NZ), 0, 8) < 7).astype(jnp.int32), jax.random.fold_in(key_list[1], 1), 0, 1)
    return dict(displacement=displacement, bond_intact=bond_intact)


bulk_modulus = 150.0
shear_modulus = 25.0
soft_stretch = 0.05

def bond_offsets():
    chosen = []
    for step_x in range(0, 4):
        for step_y in range(-3, 4):
            for step_z in range(-3, 4):
                if step_x * step_x + step_y * step_y + step_z * step_z > 9:
                    continue
                if step_x > 0 or (step_x == 0 and (step_y > 0 or (step_y == 0 and step_z > 0))):
                    chosen.append((step_x, step_y, step_z))
    return chosen

def weighted_volume():
    total = 0.0
    for offset in bond_offsets():
        squared = offset[0] * offset[0] + offset[1] * offset[1] + offset[2] * offset[2]
        total = total + math.exp(-squared / 9.0) * squared
    return 2.0 * total

def offset_terms(offset):
    squared = offset[0] * offset[0] + offset[1] * offset[1] + offset[2] * offset[2]
    return (math.sqrt(squared), math.exp(-squared / 9.0))

def bond_vector(owner_u, partner_u, offset):
    pieces = [offset[number] + partner_u[number] - owner_u[number] for number in range(3)]
    length = jnp.sqrt(pieces[0] * pieces[0] + pieces[1] * pieces[1] + pieces[2] * pieces[2])
    return (pieces, length)

def dilatation_term(length, offset, intact, volume):
    radius, weight = offset_terms(offset)
    return intact * (3.0 / volume * weight * radius) * (length - radius)

def force_scalar(length, offset, theta_owner, theta_partner, intact, volume):
    radius, weight = offset_terms(offset)
    both = theta_owner + theta_partner
    extension = length - radius
    ratio = extension / (radius * soft_stretch)
    soften = 1.0 / (1.0 + ratio * ratio)
    total = 3.0 * bulk_modulus / volume * weight * radius * both + 15.0 * shear_modulus / volume * weight * (2.0 * extension - both * (radius / 3.0))
    return intact * soften * total / length

def window(array, offset, extent):
    return array[..., 3 + offset[0]:3 + offset[0] + extent[0], 3 + offset[1]:3 + offset[1] + extent[1], 3 + offset[2]:3 + offset[2] + extent[2]]

def add_block(target, block, offset):
    starts = (0,) * (target.ndim - 3) + tuple((3 + shift_step for shift_step in offset))
    current = lax.dynamic_slice(target, starts, block.shape)
    return lax.dynamic_update_slice(target, current + block, starts)

def reference(displacement, bond_intact):
    offsets = bond_offsets()
    volume = weighted_volume()
    extent = displacement.shape[1:]
    pad_u = jnp.pad(displacement, ((0, 0), (3, 3), (3, 3), (3, 3)))
    exists = jnp.pad(jnp.ones(extent, jnp.float32), 3)
    anchor = (0, 0, 0)
    theta_sum = jnp.zeros(exists.shape, jnp.float32)
    for bond_index, offset in enumerate(offsets):
        intact = bond_intact[bond_index].astype(jnp.float32) * window(exists, offset, extent)
        pieces, length = bond_vector(displacement, window(pad_u, offset, extent), offset)
        term = dilatation_term(length, offset, intact, volume)
        theta_sum = add_block(theta_sum, term, anchor)
        theta_sum = add_block(theta_sum, term, offset)
    theta = theta_sum[3:-3, 3:-3, 3:-3]
    pad_theta = jnp.pad(theta, 3)
    force_sum = jnp.zeros((3,) + exists.shape, jnp.float32)
    for bond_index, offset in enumerate(offsets):
        intact = bond_intact[bond_index].astype(jnp.float32) * window(exists, offset, extent)
        pieces, length = bond_vector(displacement, window(pad_u, offset, extent), offset)
        scalar = force_scalar(length, offset, theta, window(pad_theta, offset, extent), intact, volume)
        push = jnp.stack([scalar * piece for piece in pieces])
        force_sum = add_block(force_sum, push, anchor)
        force_sum = add_block(force_sum, -push, offset)
    return (force_sum[:, 3:-3, 3:-3, 3:-3], theta)
```

```python
import functools
import math

import jax
import jax.numpy as jnp
from jax import lax
from jax.experimental import pallas as pl
from jax.experimental.pallas import tpu as pltpu
from jax.sharding import PartitionSpec as P

MESH = pl.DeviceIdType.MESH
bulk_modulus = 150.0
shear_modulus = 25.0
soft_stretch = 0.05
PAD = 4


def bond_offsets():
    chosen = []
    for step_x in range(0, 4):
        for step_y in range(-3, 4):
            for step_z in range(-3, 4):
                if step_x * step_x + step_y * step_y + step_z * step_z > 9:
                    continue
                if step_x > 0 or (step_x == 0 and (step_y > 0 or (step_y == 0 and step_z > 0))):
                    chosen.append((step_x, step_y, step_z))
    return chosen


def square(offset):
    return sum(step * step for step in offset)


def weighted_volume():
    return 2.0 * sum(math.exp(-square(o) / 9.0) * square(o) for o in bond_offsets())


ORDER = sorted(range(len(bond_offsets())), key=lambda k: (bond_offsets()[k][:2], bond_offsets()[k][2]))


def kernel(
    sizes, u_in, intact_hbm, force_out, theta_out,
    intact, jf, ext_s, len_s, mask, u, uz, t, tz, acc_t, acc_f, main_t, main_f,
    pack_u, pack_t, edge_t, edge_f,
    zs_u, zl_u, zh_u, yu_u, yd_u, yl_u, yh_u, pu_u, pd_u, pl_u, ph_u,
    zs_t, zl_t, zh_t, yu_t, yd_t, yl_t, yh_t, pu_t, pd_t, pl_t, ph_t,
    fx_t, fxp_t, fyu_t, fyd_t, fyl_t, fyh_t, fzs_t, fzl_t, fzh_t,
    fx_f, fxp_f, fyu_f, fyd_f, fyl_f, fyh_f, fzs_f, fzl_f, fzh_f,
    send_sem, recv_sem, load_sem,
):
    offsets = bond_offsets()
    volume = weighted_volume()
    bx, by, bz = u_in.shape[1:]
    rows = by + 2 * PAD
    per = bz // 6
    index = {a: lax.axis_index(a) for a in sizes}
    has_lo = {a: index[a] > 0 for a in sizes}
    has_hi = {a: index[a] < sizes[a] - 1 for a in sizes}
    own = slice(PAD, PAD + by)
    tiles = [slice(i, i + 8) for i in range(0, rows, 8)]

    load = pltpu.make_async_copy(intact_hbm, intact, load_sem)
    load.start()

    barrier = pltpu.get_barrier_semaphore()
    count = jnp.int32(0)
    for a in sizes:
        for has, step in ((has_lo[a], -1), (has_hi[a], 1)):
            count = count + jnp.where(has, 1, 0).astype(jnp.int32)

            @pl.when(has)
            def _(a=a, step=step):
                pl.semaphore_signal(barrier, inc=1, device_id={a: index[a] + step}, device_id_type=MESH)

    used = [0]

    class Shift:
        def __init__(self, axis, step, src, dst):
            number = used[0]
            used[0] += 1
            self.copy = pltpu.make_async_remote_copy(
                src_ref=src, dst_ref=dst, send_sem=send_sem.at[number], recv_sem=recv_sem.at[number],
                device_id={axis: index[axis] + step}, device_id_type=MESH,
            )
            self.sends = has_hi[axis] if step > 0 else has_lo[axis]
            self.takes = has_lo[axis] if step > 0 else has_hi[axis]
            self.dst = dst

            @pl.when(self.sends)
            def _():
                self.copy.start()

        def receive(self):
            @pl.when(self.takes)
            def _():
                self.copy.wait_recv()

            @pl.when(jnp.logical_not(self.takes))
            def _():
                self.dst[...] = jnp.zeros(self.dst.shape, jnp.float32)

            pending.append(self)

        def finish(self):
            @pl.when(self.sends)
            def _():
                self.copy.wait_send()

    pending = []

    lane8 = lax.broadcasted_iota(jnp.int32, (8, bz), 1)
    lane = lax.broadcasted_iota(jnp.int32, (by, bz), 1)
    row = lax.broadcasted_iota(jnp.int32, (by, bz), 0)
    edge = (lane < 3) | (lane >= bz - 3)
    first = lax.rem(lane, 6) < 3

    def place(x, c, comps):
        group = x * comps + c
        return group // per, 6 * (group % per) + 3

    def roll(value, amount):
        return pltpu.roll(value, amount % bz, 1)

    def spread_a(f, comps, zs, zl, zh, yu, yd, yl, yh):
        n = zs.shape[0]
        packed = [None] * n
        for x in range(bx):
            for c in range(comps):
                value = f[x, c, own, :]
                slot, at = place(x, c, comps)
                moved = roll(jnp.where(edge, value, 0.0), at)
                packed[slot] = moved if packed[slot] is None else packed[slot] + moved
                i = x * comps + c
                part = slice(4 * (i % 2), 4 * (i % 2) + 4)
                yu[i // 2, part, :] = f[x, c, PAD + by - 4 : PAD + by, :]
                yd[i // 2, part, :] = f[x, c, PAD : PAD + 4, :]
        for s in range(n):
            zs[s] = packed[s]

    def spread_b(zs, zl, zh, yu, yd, yl, yh):
        z = Shift("gz", 1, zs, zl), Shift("gz", -1, zs, zh)
        y = Shift("gy", 1, yu, yl), Shift("gy", -1, yd, yh)
        return z, y

    def spread_c(f, comps, pack, z, y, zl, zh, yl, yh, pu, pd, plo, phi):
        n = zl.shape[0]
        for s in z:
            s.receive()
        for s in range(n):
            pack[s, own, :] = jnp.where(first, zl[s], zh[s])
            pu[s, 0:4, :] = pack[s, PAD + by - 4 : PAD + by, :]
            pd[s, 0:4, :] = pack[s, PAD : PAD + 4, :]
            pu[s, 4:8, :] = jnp.zeros((4, bz), jnp.float32)
            pd[s, 4:8, :] = jnp.zeros((4, bz), jnp.float32)
        p = Shift("gy", 1, pu, plo), Shift("gy", -1, pd, phi)
        for s in y:
            s.receive()
        for x in range(bx):
            for c in range(comps):
                i = x * comps + c
                part = slice(4 * (i % 2), 4 * (i % 2) + 4)
                f[x, c, 0:4, :] = yl[i // 2, part, :]
                f[x, c, PAD + by : rows, :] = yh[i // 2, part, :]
        xs = Shift("gx", -1, f.at[0:3], f.at[bx : bx + 3])
        for s in p:
            s.receive()
        for s in range(n):
            pack[s, 0:4, :] = plo[s, 0:4, :]
            pack[s, PAD + by : rows, :] = phi[s, 0:4, :]
        xp = Shift("gx", -1, pack.at[0], pack.at[n])
        return xs, xp

    def shifted(f, comps, pack, out, low, high):
        n = pack.shape[0] - 1
        for x in range(low, high):
            for c in range(comps):
                slot, at = place(x, c, comps) if x < bx else (n, place(x - bx, c, comps)[1])
                for tile in tiles:
                    value = f[x, c, tile, :]
                    beyond = roll(pack[slot, tile, :], -at)
                    for s in range(-3, 4):
                        if s == 0:
                            moved = value
                        else:
                            fresh = lane8 < s if s > 0 else lane8 >= bz + s
                            moved = roll(jnp.where(fresh, beyond, value), -s)
                        if comps == 3 and c == 2 and s != 0:
                            moved = moved + float(s)
                        out[s + 3, x, c, tile, :] = moved

    def combine(acc, comps, main, edges, low, high):
        n = edges.shape[0] - 1
        total = {}
        for x in range(low, high):
            for c in range(comps):
                slot, at = place(x, c, comps) if x < bx else (n, place(x - bx, c, comps)[1])
                for i, tile in enumerate(tiles):
                    inner = acc[3, x, c, tile, :]
                    over = None
                    for s in (-3, -2, -1, 1, 2, 3):
                        moved = roll(acc[s + 3, x, c, tile, :], s)
                        wrapped = lane8 < s if s > 0 else lane8 >= bz + s
                        inner = inner + jnp.where(wrapped, 0.0, moved)
                        beyond = jnp.where(wrapped, moved, 0.0)
                        over = beyond if over is None else over + beyond
                    main[x, c, tile, :] = inner
                    over = roll(over, at)
                    total[slot, i] = over if (slot, i) not in total else total[slot, i] + over
        for (slot, i), value in total.items():
            edges[slot, tiles[i], :] = value

    def fold_x(main, edges, fx, fxp):
        n = edges.shape[0] - 1
        return Shift("gx", 1, main.at[bx : bx + 3], fx), Shift("gx", 1, edges.at[n], fxp)

    def fold_y(comps, main, edges, xs, fx, fxp, fyu, fyd, fyl, fyh):
        n = edges.shape[0] - 1
        for s in xs:
            s.receive()
        for x in range(3):
            for c in range(comps):
                for tile in tiles:
                    main[x, c, tile, :] += fx[x, c, tile, :]
        for tile in tiles:
            edges[0, tile, :] += fxp[tile, :]
        base = (bx * comps + 1) // 2
        pieces = [(main.at[x, c], i) for i, (x, c) in enumerate((x, c) for x in range(bx) for c in range(comps))]
        pieces += [(edges.at[s], 2 * base + s) for s in range(n)]
        if n % 2:
            fyu[base + n // 2, 4:8, :] = jnp.zeros((4, bz), jnp.float32)
            fyd[base + n // 2, 4:8, :] = jnp.zeros((4, bz), jnp.float32)
        for ref, i in pieces:
            part = slice(4 * (i % 2), 4 * (i % 2) + 4)
            fyu[i // 2, part, :] = ref[PAD + by : rows, :]
            fyd[i // 2, part, :] = ref[0:PAD, :]
        return (Shift("gy", 1, fyu, fyl), Shift("gy", -1, fyd, fyh)), pieces

    def fold_z(pieces, edges, ys, fyl, fyh, fzs, fzl, fzh):
        n = edges.shape[0] - 1
        for s in ys:
            s.receive()
        for ref, i in pieces[-n:]:
            part = slice(4 * (i % 2), 4 * (i % 2) + 4)
            ref[PAD : PAD + 4, :] += fyl[i // 2, part, :]
            ref[PAD + by - 4 : PAD + by, :] += fyh[i // 2, part, :]
        for s in range(n):
            fzs[s] = edges[s, own, :]
        zs = Shift("gz", 1, fzs, fzl), Shift("gz", -1, fzs, fzh)
        for ref, i in pieces[:-n]:
            part = slice(4 * (i % 2), 4 * (i % 2) + 4)
            ref[PAD : PAD + 4, :] += fyl[i // 2, part, :]
            ref[PAD + by - 4 : PAD + by, :] += fyh[i // 2, part, :]
        return zs

    def fold_end(comps, main, zs, fzl, fzh, write):
        for s in zs:
            s.receive()
        arrived = [jnp.where(first, fzh[s], fzl[s]) for s in range(fzl.shape[0])]
        for x in range(bx):
            for c in range(comps):
                slot, at = place(x, c, comps)
                beyond = jnp.where(edge, roll(arrived[slot], -at), 0.0)
                write(x, c, main[x, c, own, :] + beyond)

    for x in range(bx):
        for c in range(3):
            u[x, c, own, :] = u_in[c, x]
    spread_a(u, 3, zs_u, zl_u, zh_u, yu_u, yd_u, yl_u, yh_u)
    pl.semaphore_wait(barrier, count)
    z, y = spread_b(zs_u, zl_u, zh_u, yu_u, yd_u, yl_u, yh_u)

    pairs = sorted({o[1:] for o in offsets})
    at_y = index["gy"] * by + row
    at_z = index["gz"] * bz + lane
    for i, (ey, ez) in enumerate(pairs):
        inside = (at_y + ey >= 0) & (at_y + ey < sizes["gy"] * by) & (at_z + ez >= 0) & (at_z + ez < sizes["gz"] * bz)
        mask[i] = jnp.where(inside, 1.0, 0.0)

    def clear(acc):
        zeros = jnp.zeros(acc.shape[2:], jnp.float32)

        def body(i, carry):
            for s in range(7):
                acc[s, i] = zeros
            return carry

        lax.fori_loop(0, acc.shape[1], body, 0)

    clear(acc_t)
    load.wait()

    def prepare(x, carry):
        for k in ORDER:
            ex, ey, ez = offsets[k]
            value = intact[k, x].astype(jnp.float32) * mask[pairs.index((ey, ez))]
            if ex:
                value = value * jnp.where((x + ex < bx) | has_hi["gx"], 1.0, 0.0)
            jf[k, x] = value
        return carry

    xs = spread_c(u, 3, pack_u, z, y, zl_u, zh_u, yl_u, yh_u, pu_u, pd_u, pl_u, ph_u)
    lax.fori_loop(0, bx, prepare, 0)
    shifted(u, 3, pack_u, uz, 0, bx)
    for s in xs:
        s.receive()
    shifted(u, 3, pack_u, uz, bx, bx + 3)

    def bond(x, k, mine):
        ex, ey, ez = offsets[k]
        part = slice(PAD + ey, PAD + ey + by)
        other = [uz[ez + 3, x + ex, c, part, :] for c in range(3)]
        if ex:
            other[0] = other[0] + float(ex)
        if ey:
            other[1] = other[1] + float(ey)
        return [other[c] - mine[c] for c in range(3)], part

    def dilate(x, carry):
        mine = [u[x, c, own, :] for c in range(3)]
        total = jnp.zeros((by, bz), jnp.float32)
        for k in ORDER:
            ex, ey, ez = offsets[k]
            d, part = bond(x, k, mine)
            radius = math.sqrt(square(offsets[k]))
            weight = math.exp(-square(offsets[k]) / 9.0)
            long2 = d[0] * d[0] + d[1] * d[1] + d[2] * d[2]
            ext = long2 * lax.rsqrt(long2) - radius
            term = jf[k, x] * (3.0 / volume * weight * radius) * ext
            ext_s[k, x] = ext
            len_s[k, x] = long2
            total = total + term
            acc_t[ez + 3, x + ex, 0, part, :] += term
        acc_t[3, x, 0, own, :] += total
        return carry

    lax.fori_loop(0, bx, dilate, 0)

    def soften(part):
        def body(x, carry):
            for k in part:
                radius = math.sqrt(square(offsets[k]))
                weight = math.exp(-square(offsets[k]) / 9.0)
                ext = ext_s[k, x]
                more = 1.0 + (ext * ext) * (1.0 / (radius * soft_stretch) ** 2)
                scale = jf[k, x] * lax.rsqrt(more * more * len_s[k, x])
                a = 3.0 * bulk_modulus / volume * weight * radius
                b = 15.0 * shear_modulus / volume * weight
                len_s[k, x] = scale * (a - b * radius / 3.0)
                ext_s[k, x] = scale * ext * (2.0 * b)
            return carry

        lax.fori_loop(0, bx, body, 0)

    third = (len(ORDER) + 2) // 3
    combine(acc_t, 1, main_t, edge_t, bx, bx + 3)
    xs = fold_x(main_t, edge_t, fx_t, fxp_t)
    combine(acc_t, 1, main_t, edge_t, 0, bx)
    soften(ORDER[:third])
    ys, pieces = fold_y(1, main_t, edge_t, xs, fx_t, fxp_t, fyu_t, fyd_t, fyl_t, fyh_t)
    soften(ORDER[third : 2 * third])
    zs = fold_z(pieces, edge_t, ys, fyl_t, fyh_t, fzs_t, fzl_t, fzh_t)
    soften(ORDER[2 * third :])

    def write_theta(x, c, value):
        theta_out[x] = value
        t[x, 0, own, :] = value

    fold_end(1, main_t, zs, fzl_t, fzh_t, write_theta)
    spread_a(t, 1, zs_t, zl_t, zh_t, yu_t, yd_t, yl_t, yh_t)
    z, y = spread_b(zs_t, zl_t, zh_t, yu_t, yd_t, yl_t, yh_t)
    clear(acc_f)
    xs = spread_c(t, 1, pack_t, z, y, zl_t, zh_t, yl_t, yh_t, pu_t, pd_t, pl_t, ph_t)
    shifted(t, 1, pack_t, tz, 0, bx)
    for s in xs:
        s.receive()
    shifted(t, 1, pack_t, tz, bx, bx + 3)

    def push(x, carry):
        mine = [u[x, c, own, :] for c in range(3)]
        here = t[x, 0, own, :]
        total = [jnp.zeros((by, bz), jnp.float32) for c in range(3)]
        for k in ORDER:
            ex, ey, ez = offsets[k]
            d, part = bond(x, k, mine)
            scalar = len_s[k, x] * (here + tz[ez + 3, x + ex, 0, part, :]) + ext_s[k, x]
            for c in range(3):
                pushed = scalar * d[c]
                total[c] = total[c] + pushed
                acc_f[ez + 3, x + ex, c, part, :] -= pushed
        for c in range(3):
            acc_f[3, x, c, own, :] += total[c]
        return carry

    lax.fori_loop(0, bx, push, 0)
    combine(acc_f, 3, main_f, edge_f, bx, bx + 3)
    xs = fold_x(main_f, edge_f, fx_f, fxp_f)
    combine(acc_f, 3, main_f, edge_f, 0, bx)
    ys, pieces = fold_y(3, main_f, edge_f, xs, fx_f, fxp_f, fyu_f, fyd_f, fyl_f, fyh_f)
    zs = fold_z(pieces, edge_f, ys, fyl_f, fyh_f, fzs_f, fzl_f, fzh_f)

    def write_force(x, c, value):
        force_out[c, x] = value

    fold_end(3, main_f, zs, fzl_f, fzh_f, write_force)
    for s in pending:
        s.finish()


def shards(sizes, displacement, bond_intact):
    bx, by, bz = displacement.shape[1:]
    bonds = bond_intact.shape[0]
    rows = by + 2 * PAD
    f32 = lambda *shape: pltpu.VMEM(shape, jnp.float32)
    slots = {c: -(-bx * c // (bz // 6)) for c in (1, 3)}

    def spread_buffers(c):
        n, m = slots[c], (bx * c + 1) // 2
        return [f32(n, by, bz)] * 3 + [f32(m, 8, bz)] * 4 + [f32(n, 8, bz)] * 4

    def fold_buffers(c):
        n, m = slots[c], (bx * c + 1) // 2
        return (
            [f32(3, c, rows, bz), f32(rows, bz)]
            + [f32(m + (n + 1) // 2, 8, bz)] * 4
            + [f32(n, by, bz)] * 3
        )

    pairs = len({o[1:] for o in bond_offsets()})
    scratch = (
        [pltpu.VMEM((bonds, bx, by, bz), jnp.int32)]
        + [f32(bonds, bx, by, bz)] * 3
        + [f32(pairs, by, bz)]
        + [f32(bx + 3, 3, rows, bz), f32(7, bx + 3, 3, rows, bz)]
        + [f32(bx + 3, 1, rows, bz), f32(7, bx + 3, 1, rows, bz)]
        + [f32(7, bx + 3, 1, rows, bz), f32(7, bx + 3, 3, rows, bz)]
        + [f32(bx + 3, 1, rows, bz), f32(bx + 3, 3, rows, bz)]
        + [f32(slots[3] + 1, rows, bz), f32(slots[1] + 1, rows, bz)]
        + [f32(slots[1] + 1, rows, bz), f32(slots[3] + 1, rows, bz)]
        + spread_buffers(3) + spread_buffers(1) + fold_buffers(1) + fold_buffers(3)
        + [pltpu.SemaphoreType.DMA((28,)), pltpu.SemaphoreType.DMA((28,)), pltpu.SemaphoreType.DMA]
    )
    vmem = pl.BlockSpec(memory_space=pltpu.VMEM)
    return pl.pallas_call(
        functools.partial(kernel, sizes),
        out_shape=(
            jax.ShapeDtypeStruct(displacement.shape, jnp.float32),
            jax.ShapeDtypeStruct(displacement.shape[1:], jnp.float32),
        ),
        in_specs=[vmem, pl.BlockSpec(memory_space=pl.ANY)],
        out_specs=(vmem, vmem),
        scratch_shapes=scratch,
        compiler_params=pltpu.CompilerParams(collective_id=0, has_side_effects=True, vmem_limit_bytes=40 << 20),
    )(displacement, bond_intact)


def solution(mesh):
    sizes = {a: mesh.shape[a] for a in ("gx", "gy", "gz")}
    return jax.shard_map(
        functools.partial(shards, sizes),
        mesh=mesh,
        in_specs=(P(None, "gx", "gy", "gz"), P(None, "gx", "gy", "gz")),
        out_specs=(P(None, "gx", "gy", "gz"), P("gx", "gy", "gz")),
        check_vma=False,
    )
```

```python
import functools
import math

import jax
import jax.numpy as jnp
from jax import lax
from jax.experimental import pallas as pl
from jax.experimental.pallas import tpu as pltpu
from jax.sharding import PartitionSpec as P

MESH = pl.DeviceIdType.MESH
bulk_modulus = 150.0
shear_modulus = 25.0
soft_stretch = 0.05
PAD = 4


def bond_offsets():
    chosen = []
    for step_x in range(0, 4):
        for step_y in range(-3, 4):
            for step_z in range(-3, 4):
                if step_x * step_x + step_y * step_y + step_z * step_z > 9:
                    continue
                if step_x > 0 or (step_x == 0 and (step_y > 0 or (step_y == 0 and step_z > 0))):
                    chosen.append((step_x, step_y, step_z))
    return chosen


def square(offset):
    return sum(step * step for step in offset)


def weighted_volume():
    return 2.0 * sum(math.exp(-square(o) / 9.0) * square(o) for o in bond_offsets())


ORDER = sorted(range(len(bond_offsets())), key=lambda k: (bond_offsets()[k][:2], bond_offsets()[k][2]))


def spread_parts(c, bx, by, bz):
    n, m, mx = -(-bx * c // (bz // 6)), (bx * c + 1) // 2, (3 * c + 1) // 2
    sent = {"z": (n, by, bz), "y+": (m, 8, bz), "y-": (m, 8, bz), "c+": (n, 8, bz), "c-": (n, 8, bz)}
    taken = {}
    for dy in (-1, 0, 1):
        for dz in (-1, 0, 1):
            shape = ((c, 3, by, bz), (1, by, bz), (mx, 8, bz), (1, 8, bz))[2 * abs(dy) + abs(dz)]
            taken[1, dy, dz] = shape
            if dy or dz:
                taken[0, dy, dz] = (None, (n, by, bz), (m, 8, bz), (n, 8, bz))[2 * abs(dy) + abs(dz)]
    return sent, taken


def fold_sent(c, bx, by, bz):
    sent, taken = spread_parts(c, bx, by, bz)
    sent["x"], sent["xz"] = (c, 3, by, bz), (1, by, bz)
    for sign, dy in (("+", 1), ("-", -1)):
        sent["xy" + sign], sent["xc" + sign] = taken[1, dy, 0], taken[1, dy, 1]
    return sent


def scratch_plan(bonds, bx, by, bz):
    rows = by + 2 * PAD
    pairs = len({o[1:] for o in bond_offsets()})
    plan = {"jf": (bonds, bx, by, bz), "ext": (bonds, bx, by, bz), "len": (bonds, bx, by, bz), "mask": (pairs, by, bz)}
    plan["u_in"] = (3, bx, by, bz)
    for name, c in (("u", 3), ("t", 1)):
        sent, taken = spread_parts(c, bx, by, bz)
        n = sent["z"][0]
        plan[name, "field"] = (bx + 3, c, rows, bz)
        plan[name, "shifted"] = plan[name, "sums"] = (7, bx + 3, c, rows, bz)
        plan[name, "main"] = (bx + 3, c, rows, bz)
        plan[name, "pack"] = plan[name, "edges"] = (n + 1, rows, bz)
        for key, shape in sent.items():
            plan[name, "s", key] = shape
        for key, shape in fold_sent(c, bx, by, bz).items():
            plan[name, "fs", key] = shape
        for key, shape in taken.items():
            plan[name, "r", key] = shape
            plan[name, "fr", key] = shape
    return plan


def kernel(sizes, names, u_hbm, intact_hbm, force_out, theta_out, *scratch):
    B = dict(zip(names, scratch))
    intact, send_sem, recv_sem, load_sem = scratch[len(names) :]
    offsets = bond_offsets()
    volume = weighted_volume()
    bx, by, bz = theta_out.shape
    rows = by + 2 * PAD
    per = bz // 6
    axes = ("gx", "gy", "gz")
    index = {a: lax.axis_index(a) for a in axes}
    has = {(a, -1): index[a] > 0 for a in axes}
    has.update({(a, 1): index[a] < sizes[a] - 1 for a in axes})
    own = slice(PAD, PAD + by)
    below, above = slice(0, PAD), slice(PAD + by, rows)
    tiles = [slice(i, i + 8) for i in range(0, rows, 8)]
    jf, ext_s, len_s, mask = B["jf"], B["ext"], B["len"], B["mask"]

    def there(direction):
        found = None
        for a, step in zip(axes, direction):
            if step:
                found = has[a, step] if found is None else found & has[a, step]
        return found

    everyone = [(x, y, z) for x in (-1, 0, 1) for y in (-1, 0, 1) for z in (-1, 0, 1) if x or y or z]
    exists = {d: there(d) for d in everyone}

    def device(direction):
        return {a: index[a] + step for a, step in zip(axes, direction) if step}

    load_u = pltpu.make_async_copy(u_hbm, B["u_in"], load_sem.at[0])
    load_u.start()
    load = pltpu.make_async_copy(intact_hbm, intact, load_sem.at[1])
    load.start()
    for key, ref in B.items():
        if isinstance(key, tuple) and key[1] in ("r", "fr"):
            ref[...] = jnp.zeros(ref.shape, jnp.float32)

    barrier = pltpu.get_barrier_semaphore()
    count = jnp.int32(0)
    for d in everyone:
        count = count + jnp.where(exists[d], 1, 0).astype(jnp.int32)

        @pl.when(exists[d])
        def _(d=d):
            pl.semaphore_signal(barrier, inc=1, device_id=device(d), device_id_type=MESH)

    copies = []

    class Shift:
        def __init__(self, direction, src, dst):
            number = len(copies)
            copies.append(self)
            self.copy = pltpu.make_async_remote_copy(
                src_ref=src, dst_ref=dst, send_sem=send_sem.at[number], recv_sem=recv_sem.at[number],
                device_id=device(direction), device_id_type=MESH,
            )
            self.sends = exists[direction]
            self.takes = exists[tuple(-step for step in direction)]

            @pl.when(self.sends)
            def _():
                self.copy.start()

        def receive(self):
            @pl.when(self.takes)
            def _():
                self.copy.wait_recv()

        def finish(self):
            @pl.when(self.sends)
            def _():
                self.copy.wait_send()

    lane8 = lax.broadcasted_iota(jnp.int32, (8, bz), 1)
    lane = lax.broadcasted_iota(jnp.int32, (by, bz), 1)
    row = lax.broadcasted_iota(jnp.int32, (by, bz), 0)
    edge = (lane < 3) | (lane >= bz - 3)
    first = lax.rem(lane, 6) < 3
    first4 = lax.rem(lax.broadcasted_iota(jnp.int32, (4, bz), 1), 6) < 3
    zeros4 = jnp.zeros((4, bz), jnp.float32)

    def place(x, c, comps):
        group = x % bx * comps + c
        return group // per, 6 * (group % per) + 3

    def half(i):
        return slice(4 * (i % 2), 4 * (i % 2) + 4)

    def roll(value, amount):
        return pltpu.roll(value, amount % bz, 1)

    def planes(comps, low, high):
        return [(x, c) for x in range(low, high) for c in range(comps)]

    signs = (("+", 1), ("-", -1))

    def spread(name, comps, whole):
        field = B[name, "field"]
        z = B[name, "s", "z"]
        n = z.shape[0]
        mx = (3 * comps + 1) // 2
        packed = [None] * n
        for i, (x, c) in enumerate(planes(comps, 0, bx)):
            slot, at = place(x, c, comps)
            moved = roll(jnp.where(edge, field[x, c, own, :], 0.0), at)
            packed[slot] = moved if packed[slot] is None else packed[slot] + moved
            B[name, "s", "y+"][i // 2, half(i), :] = field[x, c, PAD + by - 4 : PAD + by, :]
            B[name, "s", "y-"][i // 2, half(i), :] = field[x, c, PAD : PAD + 4, :]
        for s in range(n):
            z[s] = packed[s]
            B[name, "s", "c+"][s, 0:4, :] = z[s, by - 4 : by, :]
            B[name, "s", "c-"][s, 0:4, :] = z[s, 0:4, :]
            B[name, "s", "c+"][s, 4:8, :] = zeros4
            B[name, "s", "c-"][s, 4:8, :] = zeros4
        return mx, whole

    def spread_send(name, mx, whole):
        sent = {}
        for far in (1, 0):
            for dy in (1, -1, 0):
                for dz in (1, -1, 0):
                    if (far, dy, dz) == (0, 0, 0):
                        continue
                    sign = "+" if dy > 0 else "-"
                    if dy and dz:
                        src = B[name, "s", "c" + sign]
                        src = src.at[0:1] if far else src
                    elif dy:
                        src = B[name, "s", "y" + sign]
                        src = src.at[0:mx] if far else src
                    elif dz:
                        src = B[name, "s", "z"]
                        src = src.at[0:1] if far else src
                    else:
                        src = whole
                    sent[far, dy, dz] = Shift((-far, dy, dz), src, B[name, "r", (far, dy, dz)])
        return sent

    def spread_take(name, comps, sent, far):
        for (f, dy, dz), copy in sent.items():
            if f == far:
                copy.receive()
        field, pack = B[name, "field"], B[name, "pack"]
        n = pack.shape[0] - 1
        R = lambda dy, dz: B[name, "r", (far, dy, dz)]
        for s in range(1 if far else n):
            to = n if far else s
            pack[to, own, :] = jnp.where(first, R(0, 1)[s], R(0, -1)[s])
            pack[to, below, :] = jnp.where(first4, R(1, 1)[s, 0:4, :], R(1, -1)[s, 0:4, :])
            pack[to, above, :] = jnp.where(first4, R(-1, 1)[s, 0:4, :], R(-1, -1)[s, 0:4, :])
        for i, (x, c) in enumerate(planes(comps, 0, 3 if far else bx)):
            to = x + bx if far else x
            if far:
                field[to, c, own, :] = R(0, 0)[c, x]
            field[to, c, below, :] = R(1, 0)[i // 2, half(i), :]
            field[to, c, above, :] = R(-1, 0)[i // 2, half(i), :]
        shifted(name, comps, *((bx, bx + 3) if far else (0, bx)))

    def shifted(name, comps, low, high):
        field, pack, out = B[name, "field"], B[name, "pack"], B[name, "shifted"]
        n = pack.shape[0] - 1
        for x, c in planes(comps, low, high):
            slot, at = place(x, c, comps)
            slot = slot if x < bx else n
            for tile in tiles:
                value = field[x, c, tile, :]
                beyond = roll(pack[slot, tile, :], -at)
                for s in range(-3, 4):
                    if s == 0:
                        moved = value
                    else:
                        fresh = lane8 < s if s > 0 else lane8 >= bz + s
                        moved = roll(jnp.where(fresh, beyond, value), -s)
                    if comps == 3 and c == 2 and s != 0:
                        moved = moved + float(s)
                    out[s + 3, x, c, tile, :] = moved

    def combine(name, comps, low, high):
        sums, main, edges = B[name, "sums"], B[name, "main"], B[name, "edges"]
        n = edges.shape[0] - 1
        total = {}
        for x, c in planes(comps, low, high):
            slot, at = place(x, c, comps)
            slot = slot if x < bx else n
            for i, tile in enumerate(tiles):
                inner = sums[3, x, c, tile, :]
                over = None
                for s in (-3, -2, -1, 1, 2, 3):
                    moved = roll(sums[s + 3, x, c, tile, :], s)
                    wrapped = lane8 < s if s > 0 else lane8 >= bz + s
                    inner = inner + jnp.where(wrapped, 0.0, moved)
                    beyond = jnp.where(wrapped, moved, 0.0)
                    over = beyond if over is None else over + beyond
                main[x, c, tile, :] = inner
                over = roll(over, at)
                total[slot, i] = over if (slot, i) not in total else total[slot, i] + over
        for (slot, i), value in total.items():
            edges[slot, tiles[i], :] = value

    def fold_send(name, comps, far):
        combine(name, comps, *((bx, bx + 3) if far else (0, bx)))
        main, edges = B[name, "main"], B[name, "edges"]
        n = edges.shape[0] - 1
        S = lambda key: B[name, "fs", ("x" + key) if far else key]
        for i, (x, c) in enumerate(planes(comps, 0, 3 if far else bx)):
            at = x + bx if far else x
            if far:
                B[name, "fs", "x"][c, x] = main[at, c, own, :]
            S("y+")[i // 2, half(i), :] = main[at, c, above, :]
            S("y-")[i // 2, half(i), :] = main[at, c, below, :]
        if (comps * (3 if far else bx)) % 2:
            for sign, _ in signs:
                S("y" + sign)[S("y" + sign).shape[0] - 1, 4:8, :] = zeros4
        for s in range(1 if far else n):
            at = n if far else s
            S("z")[s] = edges[at, own, :]
            S("c+")[s, 0:4, :] = edges[at, above, :]
            S("c-")[s, 0:4, :] = edges[at, below, :]
            S("c+")[s, 4:8, :] = zeros4
            S("c-")[s, 4:8, :] = zeros4
        sent = []
        for dy in (1, -1, 0):
            for dz in (1, -1, 0):
                if not (far or dy or dz):
                    continue
                sign = "+" if dy > 0 else "-"
                src = S("c" + sign) if dy and dz else S("y" + sign) if dy else S("z") if dz else B[name, "fs", "x"]
                sent.append(Shift((far, dy, dz), src, B[name, "fr", (far, dy, dz)]))
        return sent

    def fold_take(name, comps, sent, write):
        main = B[name, "main"]
        R = lambda far, dy, dz: B[name, "fr", (far, dy, dz)]
        for copy in sent:
            copy.receive()
        work = B[name, "edges"]
        n = work.shape[0] - 1
        for far in (0, 1):
            for s in range(1 if far else n):
                value = jnp.where(first, R(far, 0, -1)[s], R(far, 0, 1)[s])
                work[s, own, :] = work[s, own, :] + value if far else value
                work[s, PAD : PAD + 4, :] += jnp.where(first4, R(far, 1, -1)[s, 0:4, :], R(far, 1, 1)[s, 0:4, :])
                work[s, PAD + by - 4 : PAD + by, :] += jnp.where(
                    first4, R(far, -1, -1)[s, 0:4, :], R(far, -1, 1)[s, 0:4, :]
                )
        for i, (x, c) in enumerate(planes(comps, 0, bx)):
            upper, lower = R(0, 1, 0)[i // 2, half(i), :], R(0, -1, 0)[i // 2, half(i), :]
            if x < 3:
                upper = upper + R(1, 1, 0)[i // 2, half(i), :]
                lower = lower + R(1, -1, 0)[i // 2, half(i), :]
            main[x, c, PAD : PAD + 4, :] += upper
            main[x, c, PAD + by - 4 : PAD + by, :] += lower
        for x, c in planes(comps, 0, bx):
            slot, at = place(x, c, comps)
            value = main[x, c, own, :] + jnp.where(edge, roll(work[slot, own, :], -at), 0.0)
            if x < 3:
                value = value + R(1, 0, 0)[c, x]
            write(x, c, value)

    u, uz, t, tz = B["u", "field"], B["u", "shifted"], B["t", "field"], B["t", "shifted"]
    acc_t, acc_f = B["t", "sums"], B["u", "sums"]
    load_u.wait()
    for x, c in planes(3, 0, bx):
        u[x, c, own, :] = B["u_in"][c, x]
    mx, whole = spread("u", 3, B["u_in"].at[:, 0:3])
    pl.semaphore_wait(barrier, count)
    sent = spread_send("u", mx, whole)

    pairs = sorted({o[1:] for o in offsets})
    at_y = index["gy"] * by + row
    at_z = index["gz"] * bz + lane
    for i, (ey, ez) in enumerate(pairs):
        inside = (at_y + ey >= 0) & (at_y + ey < sizes["gy"] * by) & (at_z + ez >= 0) & (at_z + ez < sizes["gz"] * bz)
        mask[i] = jnp.where(inside, 1.0, 0.0)

    def clear(acc):
        zeros = jnp.zeros(acc.shape[2:], jnp.float32)

        def body(i, carry):
            for s in range(7):
                acc[s, i] = zeros
            return carry

        lax.fori_loop(0, acc.shape[1], body, 0)

    clear(acc_t)
    load.wait()

    def prepare(x, carry):
        for k in ORDER:
            ex, ey, ez = offsets[k]
            value = intact[k, x].astype(jnp.float32) * mask[pairs.index((ey, ez))]
            if ex:
                value = value * jnp.where((x + ex < bx) | has["gx", 1], 1.0, 0.0)
            jf[k, x] = value
        return carry

    lax.fori_loop(0, bx, prepare, 0)
    clear(acc_f)
    spread_take("u", 3, sent, 0)
    spread_take("u", 3, sent, 1)

    def bond(x, k, mine):
        ex, ey, ez = offsets[k]
        part = slice(PAD + ey, PAD + ey + by)
        other = [uz[ez + 3, x + ex, c, part, :] for c in range(3)]
        if ex:
            other[0] = other[0] + float(ex)
        if ey:
            other[1] = other[1] + float(ey)
        return [other[c] - mine[c] for c in range(3)], part

    def dilate(x, carry):
        mine = [u[x, c, own, :] for c in range(3)]
        total = jnp.zeros((by, bz), jnp.float32)
        for k in ORDER:
            ex, ey, ez = offsets[k]
            d, part = bond(x, k, mine)
            radius = math.sqrt(square(offsets[k]))
            weight = math.exp(-square(offsets[k]) / 9.0)
            long2 = d[0] * d[0] + d[1] * d[1] + d[2] * d[2]
            ext = long2 * lax.rsqrt(long2) - radius
            term = jf[k, x] * (3.0 / volume * weight * radius) * ext
            ext_s[k, x] = ext
            len_s[k, x] = long2
            total = total + term
            acc_t[ez + 3, x + ex, 0, part, :] += term
        acc_t[3, x, 0, own, :] += total
        return carry

    lax.fori_loop(0, bx, dilate, 0)

    def soften(part):
        def body(x, carry):
            for k in part:
                radius = math.sqrt(square(offsets[k]))
                weight = math.exp(-square(offsets[k]) / 9.0)
                ext = ext_s[k, x]
                more = 1.0 + (ext * ext) * (1.0 / (radius * soft_stretch) ** 2)
                scale = jf[k, x] * lax.rsqrt(more * more * len_s[k, x])
                a = 3.0 * bulk_modulus / volume * weight * radius
                b = 15.0 * shear_modulus / volume * weight
                len_s[k, x] = scale * (a - b * radius / 3.0)
                ext_s[k, x] = scale * ext * (2.0 * b)
            return carry

        lax.fori_loop(0, bx, body, 0)

    cut = (2 * len(ORDER)) // 3
    sent = fold_send("t", 1, 1)
    sent += fold_send("t", 1, 0)
    soften(ORDER[:cut])

    def write_theta(x, c, value):
        theta_out[x] = value
        B["t_own"][0, x] = value
        t[x, 0, own, :] = value

    fold_take("t", 1, sent, write_theta)
    mx, whole = spread("t", 1, B["t_own"].at[:, 0:3])
    sent = spread_send("t", mx, whole)
    soften(ORDER[cut:])
    spread_take("t", 1, sent, 0)
    spread_take("t", 1, sent, 1)

    def push(x, carry):
        mine = [u[x, c, own, :] for c in range(3)]
        here = t[x, 0, own, :]
        total = [jnp.zeros((by, bz), jnp.float32) for c in range(3)]
        for k in ORDER:
            ex, ey, ez = offsets[k]
            d, part = bond(x, k, mine)
            scalar = len_s[k, x] * (here + tz[ez + 3, x + ex, 0, part, :]) + ext_s[k, x]
            for c in range(3):
                pushed = scalar * d[c]
                total[c] = total[c] + pushed
                acc_f[ez + 3, x + ex, c, part, :] -= pushed
        for c in range(3):
            acc_f[3, x, c, own, :] += total[c]
        return carry

    lax.fori_loop(0, bx, push, 0)
    sent = fold_send("u", 3, 1)
    sent += fold_send("u", 3, 0)

    def write_force(x, c, value):
        force_out[c, x] = value

    fold_take("u", 3, sent, write_force)
    for copy in copies:
        copy.finish()


def shards(sizes, displacement, bond_intact):
    plan = scratch_plan(bond_intact.shape[0], *displacement.shape[1:])
    plan["t_own"] = (1,) + displacement.shape[1:]
    scratch = [pltpu.VMEM(shape, jnp.float32) for shape in plan.values()]
    scratch += [
        pltpu.VMEM(bond_intact.shape, jnp.int32),
        pltpu.SemaphoreType.DMA((68,)),
        pltpu.SemaphoreType.DMA((68,)),
        pltpu.SemaphoreType.DMA((2,)),
    ]
    vmem, anywhere = pl.BlockSpec(memory_space=pltpu.VMEM), pl.BlockSpec(memory_space=pl.ANY)
    return pl.pallas_call(
        functools.partial(kernel, sizes, tuple(plan)),
        out_shape=(
            jax.ShapeDtypeStruct(displacement.shape, jnp.float32),
            jax.ShapeDtypeStruct(displacement.shape[1:], jnp.float32),
        ),
        in_specs=[anywhere, anywhere],
        out_specs=(vmem, vmem),
        scratch_shapes=scratch,
        compiler_params=pltpu.CompilerParams(collective_id=0, has_side_effects=True, vmem_limit_bytes=63 << 20),
    )(displacement, bond_intact)


def solution(mesh):
    sizes = {a: mesh.shape[a] for a in ("gx", "gy", "gz")}
    return jax.shard_map(
        functools.partial(shards, sizes),
        mesh=mesh,
        in_specs=(P(None, "gx", "gy", "gz"), P(None, "gx", "gy", "gz")),
        out_specs=(P(None, "gx", "gy", "gz"), P("gx", "gy", "gz")),
        check_vma=False,
    )
```

```python
import functools
import math

import jax
import jax.numpy as jnp
from jax import lax
from jax.experimental import pallas as pl
from jax.experimental.pallas import tpu as pltpu
from jax.sharding import PartitionSpec as P

MESH = pl.DeviceIdType.MESH
bulk_modulus = 150.0
shear_modulus = 25.0
soft_stretch = 0.05
PAD = 4


def bond_offsets():
    chosen = []
    for step_x in range(0, 4):
        for step_y in range(-3, 4):
            for step_z in range(-3, 4):
                if step_x * step_x + step_y * step_y + step_z * step_z > 9:
                    continue
                if step_x > 0 or (step_x == 0 and (step_y > 0 or (step_y == 0 and step_z > 0))):
                    chosen.append((step_x, step_y, step_z))
    return chosen


def square(offset):
    return sum(step * step for step in offset)


def weighted_volume():
    return 2.0 * sum(math.exp(-square(o) / 9.0) * square(o) for o in bond_offsets())


ORDER = sorted(range(len(bond_offsets())), key=lambda k: (bond_offsets()[k][:2], bond_offsets()[k][2]))


def spread_parts(c, bx, by, bz):
    n, m, mx = -(-bx * c // (bz // 6)), (bx * c + 1) // 2, (3 * c + 1) // 2
    sent = {"z": (n, by, bz), "y+": (m, 8, bz), "y-": (m, 8, bz), "c+": (n, 8, bz), "c-": (n, 8, bz)}
    taken = {}
    for dy in (-1, 0, 1):
        for dz in (-1, 0, 1):
            shape = ((c, 3, by, bz), (1, by, bz), (mx, 8, bz), (1, 8, bz))[2 * abs(dy) + abs(dz)]
            taken[1, dy, dz] = shape
            if dy or dz:
                taken[0, dy, dz] = (None, (n, by, bz), (m, 8, bz), (n, 8, bz))[2 * abs(dy) + abs(dz)]
    return sent, taken


def fold_sent(c, bx, by, bz):
    sent, taken = spread_parts(c, bx, by, bz)
    sent["x"], sent["xz"] = (c, 3, by, bz), (1, by, bz)
    for sign, dy in (("+", 1), ("-", -1)):
        sent["xy" + sign], sent["xc" + sign] = taken[1, dy, 0], taken[1, dy, 1]
    return sent


def scratch_plan(bonds, bx, by, bz):
    rows = by + 2 * PAD
    pairs = len({o[1:] for o in bond_offsets()})
    plan = {"jf": (bonds, bx, by, bz), "ext": (bonds, bx, by, bz), "len": (bonds, bx, by, bz), "mask": (pairs, by, bz)}
    plan["u_in"] = (3, bx, by, bz)
    for name, c in (("u", 3), ("t", 1)):
        sent, taken = spread_parts(c, bx, by, bz)
        n = sent["z"][0]
        plan[name, "field"] = (bx + 3, c, rows, bz)
        plan[name, "shifted"] = plan[name, "sums"] = (7, bx + 3, c, rows, bz)
        plan[name, "main"] = (bx + 3, c, rows, bz)
        plan[name, "pack"] = plan[name, "edges"] = (n + 1, rows, bz)
        for key, shape in sent.items():
            plan[name, "s", key] = shape
        for key, shape in fold_sent(c, bx, by, bz).items():
            plan[name, "fs", key] = shape
        for key, shape in taken.items():
            plan[name, "r", key] = shape
            plan[name, "fr", key] = shape
    return plan


def kernel(sizes, names, u_hbm, intact_hbm, force_out, theta_out, *scratch):
    B = dict(zip(names, scratch))
    intact, send_sem, recv_sem, load_sem = scratch[len(names) :]
    offsets = bond_offsets()
    volume = weighted_volume()
    bx, by, bz = theta_out.shape
    rows = by + 2 * PAD
    per = bz // 6
    axes = ("gx", "gy", "gz")
    index = {a: lax.axis_index(a) for a in axes}
    has = {(a, -1): index[a] > 0 for a in axes}
    has.update({(a, 1): index[a] < sizes[a] - 1 for a in axes})
    own = slice(PAD, PAD + by)
    below, above = slice(0, PAD), slice(PAD + by, rows)
    tiles = [slice(i, i + 8) for i in range(0, rows, 8)]
    jf, ext_s, len_s, mask = B["jf"], B["ext"], B["len"], B["mask"]

    def there(direction):
        found = None
        for a, step in zip(axes, direction):
            if step:
                found = has[a, step] if found is None else found & has[a, step]
        return found

    everyone = [(x, y, z) for x in (-1, 0, 1) for y in (-1, 0, 1) for z in (-1, 0, 1) if x or y or z]
    exists = {d: there(d) for d in everyone}

    def device(direction):
        return {a: index[a] + step for a, step in zip(axes, direction) if step}

    load_u = pltpu.make_async_copy(u_hbm, B["u_in"], load_sem.at[0])
    load_u.start()
    load = pltpu.make_async_copy(intact_hbm, intact, load_sem.at[1])
    load.start()
    for key, ref in B.items():
        if isinstance(key, tuple) and key[1] in ("r", "fr"):
            ref[...] = jnp.zeros(ref.shape, jnp.float32)

    barrier = pltpu.get_barrier_semaphore()
    count = jnp.int32(0)
    for d in everyone:
        count = count + jnp.where(exists[d], 1, 0).astype(jnp.int32)

        @pl.when(exists[d])
        def _(d=d):
            pl.semaphore_signal(barrier, inc=1, device_id=device(d), device_id_type=MESH)

    copies = []

    class Shift:
        def __init__(self, direction, src, dst):
            number = len(copies)
            copies.append(self)
            self.copy = pltpu.make_async_remote_copy(
                src_ref=src, dst_ref=dst, send_sem=send_sem.at[number], recv_sem=recv_sem.at[number],
                device_id=device(direction), device_id_type=MESH,
            )
            self.sends = exists[direction]
            self.takes = exists[tuple(-step for step in direction)]

            @pl.when(self.sends)
            def _():
                self.copy.start()

        def receive(self):
            @pl.when(self.takes)
            def _():
                self.copy.wait_recv()

        def finish(self):
            @pl.when(self.sends)
            def _():
                self.copy.wait_send()

    lane8 = lax.broadcasted_iota(jnp.int32, (8, bz), 1)
    lane = lax.broadcasted_iota(jnp.int32, (by, bz), 1)
    row = lax.broadcasted_iota(jnp.int32, (by, bz), 0)
    edge = (lane < 3) | (lane >= bz - 3)
    first = lax.rem(lane, 6) < 3
    first4 = lax.rem(lax.broadcasted_iota(jnp.int32, (4, bz), 1), 6) < 3
    zeros4 = jnp.zeros((4, bz), jnp.float32)

    def place(x, c, comps):
        group = x % bx * comps + c
        return group // per, 6 * (group % per) + 3

    def half(i):
        return slice(4 * (i % 2), 4 * (i % 2) + 4)

    def roll(value, amount):
        return pltpu.roll(value, amount % bz, 1)

    def planes(comps, low, high):
        return [(x, c) for x in range(low, high) for c in range(comps)]

    signs = (("+", 1), ("-", -1))

    def spread(name, comps, whole):
        field = B[name, "field"]
        z = B[name, "s", "z"]
        n = z.shape[0]
        mx = (3 * comps + 1) // 2
        packed = [None] * n
        for i, (x, c) in enumerate(planes(comps, 0, bx)):
            slot, at = place(x, c, comps)
            moved = roll(jnp.where(edge, field[x, c, own, :], 0.0), at)
            packed[slot] = moved if packed[slot] is None else packed[slot] + moved
            B[name, "s", "y+"][i // 2, half(i), :] = field[x, c, PAD + by - 4 : PAD + by, :]
            B[name, "s", "y-"][i // 2, half(i), :] = field[x, c, PAD : PAD + 4, :]
        for s in range(n):
            z[s] = packed[s]
            B[name, "s", "c+"][s, 0:4, :] = z[s, by - 4 : by, :]
            B[name, "s", "c-"][s, 0:4, :] = z[s, 0:4, :]
            B[name, "s", "c+"][s, 4:8, :] = zeros4
            B[name, "s", "c-"][s, 4:8, :] = zeros4
        return mx, whole

    def spread_send(name, mx, whole):
        sent = {}
        for far in (1, 0):
            for dy in (1, -1, 0):
                for dz in (1, -1, 0):
                    if (far, dy, dz) == (0, 0, 0):
                        continue
                    sign = "+" if dy > 0 else "-"
                    if dy and dz:
                        src = B[name, "s", "c" + sign]
                        src = src.at[0:1] if far else src
                    elif dy:
                        src = B[name, "s", "y" + sign]
                        src = src.at[0:mx] if far else src
                    elif dz:
                        src = B[name, "s", "z"]
                        src = src.at[0:1] if far else src
                    else:
                        src = whole
                    sent[far, dy, dz] = Shift((-far, dy, dz), src, B[name, "r", (far, dy, dz)])
        return sent

    def spread_take(name, comps, sent, far):
        for (f, dy, dz), copy in sent.items():
            if f == far:
                copy.receive()
        field, pack = B[name, "field"], B[name, "pack"]
        n = pack.shape[0] - 1
        R = lambda dy, dz: B[name, "r", (far, dy, dz)]
        for s in range(1 if far else n):
            to = n if far else s
            pack[to, own, :] = jnp.where(first, R(0, 1)[s], R(0, -1)[s])
            pack[to, below, :] = jnp.where(first4, R(1, 1)[s, 0:4, :], R(1, -1)[s, 0:4, :])
            pack[to, above, :] = jnp.where(first4, R(-1, 1)[s, 0:4, :], R(-1, -1)[s, 0:4, :])
        for i, (x, c) in enumerate(planes(comps, 0, 3 if far else bx)):
            to = x + bx if far else x
            if far:
                field[to, c, own, :] = R(0, 0)[c, x]
            field[to, c, below, :] = R(1, 0)[i // 2, half(i), :]
            field[to, c, above, :] = R(-1, 0)[i // 2, half(i), :]
        shifted(name, comps, *((bx, bx + 3) if far else (0, bx)))

    def shifted(name, comps, low, high):
        field, pack, out = B[name, "field"], B[name, "pack"], B[name, "shifted"]
        n = pack.shape[0] - 1
        for x, c in planes(comps, low, high):
            slot, at = place(x, c, comps)
            slot = slot if x < bx else n
            for tile in tiles:
                value = field[x, c, tile, :]
                beyond = roll(pack[slot, tile, :], -at)
                for s in range(-3, 4):
                    if s == 0:
                        moved = value
                    else:
                        fresh = lane8 < s if s > 0 else lane8 >= bz + s
                        moved = roll(jnp.where(fresh, beyond, value), -s)
                    if comps == 3 and c == 2 and s != 0:
                        moved = moved + float(s)
                    out[s + 3, x, c, tile, :] = moved

    def combine(name, comps, low, high):
        sums, main, edges = B[name, "sums"], B[name, "main"], B[name, "edges"]
        n = edges.shape[0] - 1
        total = {}
        for x, c in planes(comps, low, high):
            slot, at = place(x, c, comps)
            slot = slot if x < bx else n
            for i, tile in enumerate(tiles):
                inner = sums[3, x, c, tile, :]
                over = None
                for s in (-3, -2, -1, 1, 2, 3):
                    moved = roll(sums[s + 3, x, c, tile, :], s)
                    wrapped = lane8 < s if s > 0 else lane8 >= bz + s
                    inner = inner + jnp.where(wrapped, 0.0, moved)
                    beyond = jnp.where(wrapped, moved, 0.0)
                    over = beyond if over is None else over + beyond
                main[x, c, tile, :] = inner
                over = roll(over, at)
                total[slot, i] = over if (slot, i) not in total else total[slot, i] + over
        for (slot, i), value in total.items():
            edges[slot, tiles[i], :] = value

    def fold_send(name, comps, far):
        combine(name, comps, *((bx, bx + 3) if far else (0, bx)))
        main, edges = B[name, "main"], B[name, "edges"]
        n = edges.shape[0] - 1
        S = lambda key: B[name, "fs", ("x" + key) if far else key]
        for i, (x, c) in enumerate(planes(comps, 0, 3 if far else bx)):
            at = x + bx if far else x
            if far:
                B[name, "fs", "x"][c, x] = main[at, c, own, :]
            S("y+")[i // 2, half(i), :] = main[at, c, above, :]
            S("y-")[i // 2, half(i), :] = main[at, c, below, :]
        if (comps * (3 if far else bx)) % 2:
            for sign, _ in signs:
                S("y" + sign)[S("y" + sign).shape[0] - 1, 4:8, :] = zeros4
        for s in range(1 if far else n):
            at = n if far else s
            S("z")[s] = edges[at, own, :]
            S("c+")[s, 0:4, :] = edges[at, above, :]
            S("c-")[s, 0:4, :] = edges[at, below, :]
            S("c+")[s, 4:8, :] = zeros4
            S("c-")[s, 4:8, :] = zeros4
        sent = []
        for dy in (1, -1, 0):
            for dz in (1, -1, 0):
                if not (far or dy or dz):
                    continue
                sign = "+" if dy > 0 else "-"
                src = S("c" + sign) if dy and dz else S("y" + sign) if dy else S("z") if dz else B[name, "fs", "x"]
                sent.append(Shift((far, dy, dz), src, B[name, "fr", (far, dy, dz)]))
        return sent

    def fold_take(name, comps, sent, write):
        main = B[name, "main"]
        R = lambda far, dy, dz: B[name, "fr", (far, dy, dz)]
        for copy in sent:
            copy.receive()
        work = B[name, "edges"]
        n = work.shape[0] - 1
        for far in (0, 1):
            for s in range(1 if far else n):
                value = jnp.where(first, R(far, 0, -1)[s], R(far, 0, 1)[s])
                work[s, own, :] = work[s, own, :] + value if far else value
                work[s, PAD : PAD + 4, :] += jnp.where(first4, R(far, 1, -1)[s, 0:4, :], R(far, 1, 1)[s, 0:4, :])
                work[s, PAD + by - 4 : PAD + by, :] += jnp.where(
                    first4, R(far, -1, -1)[s, 0:4, :], R(far, -1, 1)[s, 0:4, :]
                )
        for i, (x, c) in enumerate(planes(comps, 0, bx)):
            upper, lower = R(0, 1, 0)[i // 2, half(i), :], R(0, -1, 0)[i // 2, half(i), :]
            if x < 3:
                upper = upper + R(1, 1, 0)[i // 2, half(i), :]
                lower = lower + R(1, -1, 0)[i // 2, half(i), :]
            main[x, c, PAD : PAD + 4, :] += upper
            main[x, c, PAD + by - 4 : PAD + by, :] += lower
        for x, c in planes(comps, 0, bx):
            slot, at = place(x, c, comps)
            value = main[x, c, own, :] + jnp.where(edge, roll(work[slot, own, :], -at), 0.0)
            if x < 3:
                value = value + R(1, 0, 0)[c, x]
            write(x, c, value)

    u, uz, t, tz = B["u", "field"], B["u", "shifted"], B["t", "field"], B["t", "shifted"]
    acc_t, acc_f = B["t", "sums"], B["u", "sums"]
    load_u.wait()
    for x, c in planes(3, 0, bx):
        u[x, c, own, :] = B["u_in"][c, x]
    mx, whole = spread("u", 3, B["u_in"].at[:, 0:3])
    pl.semaphore_wait(barrier, count)
    sent = spread_send("u", mx, whole)

    pairs = sorted({o[1:] for o in offsets})
    at_y = index["gy"] * by + row
    at_z = index["gz"] * bz + lane
    for i, (ey, ez) in enumerate(pairs):
        inside = (at_y + ey >= 0) & (at_y + ey < sizes["gy"] * by) & (at_z + ez >= 0) & (at_z + ez < sizes["gz"] * bz)
        mask[i] = jnp.where(inside, 1.0, 0.0)

    def clear(acc):
        zeros = jnp.zeros(acc.shape[2:], jnp.float32)

        def body(i, carry):
            for s in range(7):
                acc[s, i] = zeros
            return carry

        lax.fori_loop(0, acc.shape[1], body, 0)

    clear(acc_t)
    load.wait()

    def prepare(x, carry):
        for k in ORDER:
            ex, ey, ez = offsets[k]
            value = intact[k, x].astype(jnp.float32) * mask[pairs.index((ey, ez))]
            if ex:
                value = value * jnp.where((x + ex < bx) | has["gx", 1], 1.0, 0.0)
            jf[k, x] = value
        return carry

    lax.fori_loop(0, bx, prepare, 0)
    clear(acc_f)
    spread_take("u", 3, sent, 0)
    spread_take("u", 3, sent, 1)

    def bond(x, k, mine):
        ex, ey, ez = offsets[k]
        part = slice(PAD + ey, PAD + ey + by)
        other = [uz[ez + 3, x + ex, c, part, :] for c in range(3)]
        if ex:
            other[0] = other[0] + float(ex)
        if ey:
            other[1] = other[1] + float(ey)
        return [other[c] - mine[c] for c in range(3)], part

    def dilate(x, carry):
        mine = [u[x, c, own, :] for c in range(3)]
        total = jnp.zeros((by, bz), jnp.float32)
        for k in ORDER:
            ex, ey, ez = offsets[k]
            d, part = bond(x, k, mine)
            radius = math.sqrt(square(offsets[k]))
            weight = math.exp(-square(offsets[k]) / 9.0)
            long2 = d[0] * d[0] + d[1] * d[1] + d[2] * d[2]
            ext = long2 * lax.rsqrt(long2) - radius
            term = jf[k, x] * (3.0 / volume * weight * radius) * ext
            ext_s[k, x] = ext
            len_s[k, x] = long2
            total = total + term
            acc_t[ez + 3, x + ex, 0, part, :] += term
        acc_t[3, x, 0, own, :] += total
        return carry

    def sweep(work, name, comps):
        lax.fori_loop(0, 3, lambda i, carry: work(bx - 1 - i, carry), 0)
        sent = fold_send(name, comps, 1)
        lax.fori_loop(0, bx - 3, lambda i, carry: work(bx - 4 - i, carry), 0)
        return sent + fold_send(name, comps, 0)

    def soften(part):
        def body(x, carry):
            for k in part:
                radius = math.sqrt(square(offsets[k]))
                weight = math.exp(-square(offsets[k]) / 9.0)
                ext = ext_s[k, x]
                more = 1.0 + (ext * ext) * (1.0 / (radius * soft_stretch) ** 2)
                scale = jf[k, x] * lax.rsqrt(more * more * len_s[k, x])
                a = 3.0 * bulk_modulus / volume * weight * radius
                b = 15.0 * shear_modulus / volume * weight
                len_s[k, x] = scale * (a - b * radius / 3.0)
                ext_s[k, x] = scale * ext * (2.0 * b)
            return carry

        lax.fori_loop(0, bx, body, 0)

    cut = (2 * len(ORDER)) // 3
    sent = sweep(dilate, "t", 1)
    soften(ORDER[:cut])

    def write_theta(x, c, value):
        theta_out[x] = value
        B["t_own"][0, x] = value
        t[x, 0, own, :] = value

    fold_take("t", 1, sent, write_theta)
    mx, whole = spread("t", 1, B["t_own"].at[:, 0:3])
    sent = spread_send("t", mx, whole)
    soften(ORDER[cut:])
    spread_take("t", 1, sent, 0)
    spread_take("t", 1, sent, 1)

    def push(x, carry):
        mine = [u[x, c, own, :] for c in range(3)]
        here = t[x, 0, own, :]
        total = [jnp.zeros((by, bz), jnp.float32) for c in range(3)]
        for k in ORDER:
            ex, ey, ez = offsets[k]
            d, part = bond(x, k, mine)
            scalar = len_s[k, x] * (here + tz[ez + 3, x + ex, 0, part, :]) + ext_s[k, x]
            for c in range(3):
                pushed = scalar * d[c]
                total[c] = total[c] + pushed
                acc_f[ez + 3, x + ex, c, part, :] -= pushed
        for c in range(3):
            acc_f[3, x, c, own, :] += total[c]
        return carry

    sent = sweep(push, "u", 3)

    def write_force(x, c, value):
        force_out[c, x] = value

    fold_take("u", 3, sent, write_force)
    for copy in copies:
        copy.finish()


def shards(sizes, displacement, bond_intact):
    plan = scratch_plan(bond_intact.shape[0], *displacement.shape[1:])
    plan["t_own"] = (1,) + displacement.shape[1:]
    scratch = [pltpu.VMEM(shape, jnp.float32) for shape in plan.values()]
    scratch += [
        pltpu.VMEM(bond_intact.shape, jnp.int32),
        pltpu.SemaphoreType.DMA((68,)),
        pltpu.SemaphoreType.DMA((68,)),
        pltpu.SemaphoreType.DMA((2,)),
    ]
    vmem, anywhere = pl.BlockSpec(memory_space=pltpu.VMEM), pl.BlockSpec(memory_space=pl.ANY)
    return pl.pallas_call(
        functools.partial(kernel, sizes, tuple(plan)),
        out_shape=(
            jax.ShapeDtypeStruct(displacement.shape, jnp.float32),
            jax.ShapeDtypeStruct(displacement.shape[1:], jnp.float32),
        ),
        in_specs=[anywhere, anywhere],
        out_specs=(vmem, vmem),
        scratch_shapes=scratch,
        compiler_params=pltpu.CompilerParams(collective_id=0, has_side_effects=True, vmem_limit_bytes=63 << 20),
    )(displacement, bond_intact)


def solution(mesh):
    sizes = {a: mesh.shape[a] for a in ("gx", "gy", "gz")}
    return jax.shard_map(
        functools.partial(shards, sizes),
        mesh=mesh,
        in_specs=(P(None, "gx", "gy", "gz"), P(None, "gx", "gy", "gz")),
        out_specs=(P(None, "gx", "gy", "gz"), P("gx", "gy", "gz")),
        check_vma=False,
    )
```

```python
import functools
import math

import jax
import jax.numpy as jnp
from jax import lax
from jax.experimental import pallas as pl
from jax.experimental.pallas import tpu as pltpu
from jax.sharding import PartitionSpec as P

MESH = pl.DeviceIdType.MESH
bulk_modulus = 150.0
shear_modulus = 25.0
soft_stretch = 0.05
PAD = 4


def bond_offsets():
    chosen = []
    for step_x in range(0, 4):
        for step_y in range(-3, 4):
            for step_z in range(-3, 4):
                if step_x * step_x + step_y * step_y + step_z * step_z > 9:
                    continue
                if step_x > 0 or (step_x == 0 and (step_y > 0 or (step_y == 0 and step_z > 0))):
                    chosen.append((step_x, step_y, step_z))
    return chosen


def square(offset):
    return sum(step * step for step in offset)


def weighted_volume():
    return 2.0 * sum(math.exp(-square(o) / 9.0) * square(o) for o in bond_offsets())


ORDER = sorted(range(len(bond_offsets())), key=lambda k: (bond_offsets()[k][:2], bond_offsets()[k][2]))


def spread_parts(c, bx, by, bz):
    n, m, mx = -(-bx * c // (bz // 6)), (bx * c + 1) // 2, (3 * c + 1) // 2
    sent = {"z": (n, by, bz), "y+": (m, 8, bz), "y-": (m, 8, bz), "c+": (n, 8, bz), "c-": (n, 8, bz)}
    taken = {}
    for dy in (-1, 0, 1):
        for dz in (-1, 0, 1):
            shape = ((c, 3, by, bz), (1, by, bz), (mx, 8, bz), (1, 8, bz))[2 * abs(dy) + abs(dz)]
            taken[1, dy, dz] = shape
            if dy or dz:
                taken[0, dy, dz] = (None, (n, by, bz), (m, 8, bz), (n, 8, bz))[2 * abs(dy) + abs(dz)]
    return sent, taken


def fold_sent(c, bx, by, bz):
    sent, taken = spread_parts(c, bx, by, bz)
    sent["x"], sent["xz"] = (c, 3, by, bz), (1, by, bz)
    for sign, dy in (("+", 1), ("-", -1)):
        sent["xy" + sign], sent["xc" + sign] = taken[1, dy, 0], taken[1, dy, 1]
    return sent


def scratch_plan(bonds, bx, by, bz):
    rows = by + 2 * PAD
    pairs = len({o[1:] for o in bond_offsets()})
    plan = {"jf": (bonds, bx, by, bz), "ext": (bonds, bx, by, bz), "len": (bonds, bx, by, bz), "mask": (pairs, by, bz)}
    plan["u_in"] = (3, bx, by, bz)
    for name, c in (("u", 3), ("t", 1)):
        sent, taken = spread_parts(c, bx, by, bz)
        n = sent["z"][0]
        plan[name, "field"] = (bx + 3, c, rows, bz)
        plan[name, "shifted"] = plan[name, "sums"] = (7, bx + 3, c, rows, bz)
        plan[name, "main"] = (bx + 3, c, rows, bz)
        plan[name, "pack"] = plan[name, "edges"] = (n + 1, rows, bz)
        for key, shape in sent.items():
            plan[name, "s", key] = shape
        for key, shape in fold_sent(c, bx, by, bz).items():
            plan[name, "fs", key] = shape
        for key, shape in taken.items():
            plan[name, "r", key] = shape
            plan[name, "fr", key] = shape
    return plan


def kernel(sizes, names, u_hbm, intact_hbm, force_out, theta_out, *scratch):
    B = dict(zip(names, scratch))
    intact, send_sem, recv_sem, load_sem = scratch[len(names) :]
    offsets = bond_offsets()
    volume = weighted_volume()
    bx, by, bz = theta_out.shape
    rows = by + 2 * PAD
    per = bz // 6
    axes = ("gx", "gy", "gz")
    index = {a: lax.axis_index(a) for a in axes}
    has = {(a, -1): index[a] > 0 for a in axes}
    has.update({(a, 1): index[a] < sizes[a] - 1 for a in axes})
    own = slice(PAD, PAD + by)
    below, above = slice(0, PAD), slice(PAD + by, rows)
    tiles = [slice(i, i + 8) for i in range(0, rows, 8)]
    jf, ext_s, len_s, mask = B["jf"], B["ext"], B["len"], B["mask"]

    def there(direction):
        found = None
        for a, step in zip(axes, direction):
            if step:
                found = has[a, step] if found is None else found & has[a, step]
        return found

    everyone = [(x, y, z) for x in (-1, 0, 1) for y in (-1, 0, 1) for z in (-1, 0, 1) if x or y or z]
    exists = {d: there(d) for d in everyone}

    def device(direction):
        return {a: index[a] + step for a, step in zip(axes, direction) if step}

    load_u = pltpu.make_async_copy(u_hbm, B["u_in"], load_sem.at[0])
    load_u.start()
    load = pltpu.make_async_copy(intact_hbm, intact, load_sem.at[1])
    load.start()
    for key, ref in B.items():
        if isinstance(key, tuple) and key[1] in ("r", "fr"):
            ref[...] = jnp.zeros(ref.shape, jnp.float32)

    barrier = pltpu.get_barrier_semaphore()
    count = jnp.int32(0)
    for d in everyone:
        count = count + jnp.where(exists[d], 1, 0).astype(jnp.int32)

        @pl.when(exists[d])
        def _(d=d):
            pl.semaphore_signal(barrier, inc=1, device_id=device(d), device_id_type=MESH)

    copies = []

    class Shift:
        def __init__(self, direction, src, dst):
            number = len(copies)
            copies.append(self)
            self.copy = pltpu.make_async_remote_copy(
                src_ref=src, dst_ref=dst, send_sem=send_sem.at[number], recv_sem=recv_sem.at[number],
                device_id=device(direction), device_id_type=MESH,
            )
            self.sends = exists[direction]
            self.takes = exists[tuple(-step for step in direction)]

            @pl.when(self.sends)
            def _():
                self.copy.start()

        def receive(self):
            @pl.when(self.takes)
            def _():
                self.copy.wait_recv()

        def finish(self):
            @pl.when(self.sends)
            def _():
                self.copy.wait_send()

    lane8 = lax.broadcasted_iota(jnp.int32, (8, bz), 1)
    lane = lax.broadcasted_iota(jnp.int32, (by, bz), 1)
    row = lax.broadcasted_iota(jnp.int32, (by, bz), 0)
    edge = (lane < 3) | (lane >= bz - 3)
    first = lax.rem(lane, 6) < 3
    first4 = lax.rem(lax.broadcasted_iota(jnp.int32, (4, bz), 1), 6) < 3
    zeros4 = jnp.zeros((4, bz), jnp.float32)

    def place(x, c, comps):
        group = x % bx * comps + c
        return group // per, 6 * (group % per) + 3

    def half(i):
        return slice(4 * (i % 2), 4 * (i % 2) + 4)

    def roll(value, amount):
        return pltpu.roll(value, amount % bz, 1)

    def planes(comps, low, high):
        return [(x, c) for x in range(low, high) for c in range(comps)]

    signs = (("+", 1), ("-", -1))

    def spread(name, comps, whole):
        field = B[name, "field"]
        z = B[name, "s", "z"]
        n = z.shape[0]
        mx = (3 * comps + 1) // 2
        packed = [None] * n
        for i, (x, c) in enumerate(planes(comps, 0, bx)):
            slot, at = place(x, c, comps)
            moved = roll(jnp.where(edge, field[x, c, own, :], 0.0), at)
            packed[slot] = moved if packed[slot] is None else packed[slot] + moved
            B[name, "s", "y+"][i // 2, half(i), :] = field[x, c, PAD + by - 4 : PAD + by, :]
            B[name, "s", "y-"][i // 2, half(i), :] = field[x, c, PAD : PAD + 4, :]
        for s in range(n):
            z[s] = packed[s]
            B[name, "s", "c+"][s, 0:4, :] = z[s, by - 4 : by, :]
            B[name, "s", "c-"][s, 0:4, :] = z[s, 0:4, :]
            B[name, "s", "c+"][s, 4:8, :] = zeros4
            B[name, "s", "c-"][s, 4:8, :] = zeros4
        return mx, whole

    def spread_send(name, mx, whole):
        sent = {}
        for far in (1, 0):
            for dy in (1, -1, 0):
                for dz in (1, -1, 0):
                    if (far, dy, dz) == (0, 0, 0):
                        continue
                    sign = "+" if dy > 0 else "-"
                    if dy and dz:
                        src = B[name, "s", "c" + sign]
                        src = src.at[0:1] if far else src
                    elif dy:
                        src = B[name, "s", "y" + sign]
                        src = src.at[0:mx] if far else src
                    elif dz:
                        src = B[name, "s", "z"]
                        src = src.at[0:1] if far else src
                    else:
                        src = whole
                    sent[far, dy, dz] = Shift((-far, dy, dz), src, B[name, "r", (far, dy, dz)])
        return sent

    def spread_take(name, comps, sent, far):
        for (f, dy, dz), copy in sent.items():
            if f == far:
                copy.receive()
        field, pack = B[name, "field"], B[name, "pack"]
        n = pack.shape[0] - 1
        R = lambda dy, dz: B[name, "r", (far, dy, dz)]
        for s in range(1 if far else n):
            to = n if far else s
            pack[to, own, :] = jnp.where(first, R(0, 1)[s], R(0, -1)[s])
            pack[to, below, :] = jnp.where(first4, R(1, 1)[s, 0:4, :], R(1, -1)[s, 0:4, :])
            pack[to, above, :] = jnp.where(first4, R(-1, 1)[s, 0:4, :], R(-1, -1)[s, 0:4, :])
        for i, (x, c) in enumerate(planes(comps, 0, 3 if far else bx)):
            to = x + bx if far else x
            if far:
                field[to, c, own, :] = R(0, 0)[c, x]
            field[to, c, below, :] = R(1, 0)[i // 2, half(i), :]
            field[to, c, above, :] = R(-1, 0)[i // 2, half(i), :]
        shifted(name, comps, *((bx, bx + 3) if far else (0, bx)))

    def shifted(name, comps, low, high):
        field, pack, out = B[name, "field"], B[name, "pack"], B[name, "shifted"]
        n = pack.shape[0] - 1
        for x, c in planes(comps, low, high):
            slot, at = place(x, c, comps)
            slot = slot if x < bx else n
            for tile in tiles:
                value = field[x, c, tile, :]
                beyond = roll(pack[slot, tile, :], -at)
                for s in range(-3, 4):
                    if s == 0:
                        moved = value
                    else:
                        fresh = lane8 < s if s > 0 else lane8 >= bz + s
                        moved = roll(jnp.where(fresh, beyond, value), -s)
                    if comps == 3 and c == 2 and s != 0:
                        moved = moved + float(s)
                    out[s + 3, x, c, tile, :] = moved

    def combine(name, comps, low, high):
        sums, main, edges = B[name, "sums"], B[name, "main"], B[name, "edges"]
        n = edges.shape[0] - 1
        total = {}
        for x, c in planes(comps, low, high):
            slot, at = place(x, c, comps)
            slot = slot if x < bx else n
            for i, tile in enumerate(tiles):
                inner = sums[3, x, c, tile, :]
                over = None
                for s in (-3, -2, -1, 1, 2, 3):
                    moved = roll(sums[s + 3, x, c, tile, :], s)
                    wrapped = lane8 < s if s > 0 else lane8 >= bz + s
                    inner = inner + jnp.where(wrapped, 0.0, moved)
                    beyond = jnp.where(wrapped, moved, 0.0)
                    over = beyond if over is None else over + beyond
                main[x, c, tile, :] = inner
                over = roll(over, at)
                total[slot, i] = over if (slot, i) not in total else total[slot, i] + over
        for (slot, i), value in total.items():
            edges[slot, tiles[i], :] = value

    def fold_send(name, comps, far):
        combine(name, comps, *((bx, bx + 3) if far else (0, bx)))
        main, edges = B[name, "main"], B[name, "edges"]
        n = edges.shape[0] - 1
        S = lambda key: B[name, "fs", ("x" + key) if far else key]
        for i, (x, c) in enumerate(planes(comps, 0, 3 if far else bx)):
            at = x + bx if far else x
            if far:
                B[name, "fs", "x"][c, x] = main[at, c, own, :]
            S("y+")[i // 2, half(i), :] = main[at, c, above, :]
            S("y-")[i // 2, half(i), :] = main[at, c, below, :]
        if (comps * (3 if far else bx)) % 2:
            for sign, _ in signs:
                S("y" + sign)[S("y" + sign).shape[0] - 1, 4:8, :] = zeros4
        for s in range(1 if far else n):
            at = n if far else s
            S("z")[s] = edges[at, own, :]
            S("c+")[s, 0:4, :] = edges[at, above, :]
            S("c-")[s, 0:4, :] = edges[at, below, :]
            S("c+")[s, 4:8, :] = zeros4
            S("c-")[s, 4:8, :] = zeros4
        sent = []
        for dy in (1, -1, 0):
            for dz in (1, -1, 0):
                if not (far or dy or dz):
                    continue
                sign = "+" if dy > 0 else "-"
                src = S("c" + sign) if dy and dz else S("y" + sign) if dy else S("z") if dz else B[name, "fs", "x"]
                sent.append(Shift((far, dy, dz), src, B[name, "fr", (far, dy, dz)]))
        return sent

    def fold_take(name, comps, sent, write):
        main = B[name, "main"]
        R = lambda far, dy, dz: B[name, "fr", (far, dy, dz)]
        for copy in sent:
            copy.receive()
        work = B[name, "edges"]
        n = work.shape[0] - 1
        for far in (0, 1):
            for s in range(1 if far else n):
                value = jnp.where(first, R(far, 0, -1)[s], R(far, 0, 1)[s])
                work[s, own, :] = work[s, own, :] + value if far else value
                work[s, PAD : PAD + 4, :] += jnp.where(first4, R(far, 1, -1)[s, 0:4, :], R(far, 1, 1)[s, 0:4, :])
                work[s, PAD + by - 4 : PAD + by, :] += jnp.where(
                    first4, R(far, -1, -1)[s, 0:4, :], R(far, -1, 1)[s, 0:4, :]
                )
        for i, (x, c) in enumerate(planes(comps, 0, bx)):
            upper, lower = R(0, 1, 0)[i // 2, half(i), :], R(0, -1, 0)[i // 2, half(i), :]
            if x < 3:
                upper = upper + R(1, 1, 0)[i // 2, half(i), :]
                lower = lower + R(1, -1, 0)[i // 2, half(i), :]
            main[x, c, PAD : PAD + 4, :] += upper
            main[x, c, PAD + by - 4 : PAD + by, :] += lower
        for x, c in planes(comps, 0, bx):
            slot, at = place(x, c, comps)
            value = main[x, c, own, :] + jnp.where(edge, roll(work[slot, own, :], -at), 0.0)
            if x < 3:
                value = value + R(1, 0, 0)[c, x]
            write(x, c, value)

    u, uz, t, tz = B["u", "field"], B["u", "shifted"], B["t", "field"], B["t", "shifted"]
    acc_t, acc_f = B["t", "sums"], B["u", "sums"]
    load_u.wait()
    for x, c in planes(3, 0, bx):
        u[x, c, own, :] = B["u_in"][c, x]
    mx, whole = spread("u", 3, B["u_in"].at[:, 0:3])
    pl.semaphore_wait(barrier, count)
    sent = spread_send("u", mx, whole)

    pairs = sorted({o[1:] for o in offsets})
    at_y = index["gy"] * by + row
    at_z = index["gz"] * bz + lane
    for i, (ey, ez) in enumerate(pairs):
        inside = (at_y + ey >= 0) & (at_y + ey < sizes["gy"] * by) & (at_z + ez >= 0) & (at_z + ez < sizes["gz"] * bz)
        mask[i] = jnp.where(inside, 1.0, 0.0)

    def clear(acc):
        zeros = jnp.zeros(acc.shape[2:], jnp.float32)

        def body(i, carry):
            for s in range(7):
                acc[s, i] = zeros
            return carry

        lax.fori_loop(0, acc.shape[1], body, 0)

    clear(acc_t)
    load.wait()

    def prepare(x, carry):
        for k in ORDER:
            ex, ey, ez = offsets[k]
            value = intact[k, x].astype(jnp.float32) * mask[pairs.index((ey, ez))]
            if ex:
                value = value * jnp.where((x + ex < bx) | has["gx", 1], 1.0, 0.0)
            jf[k, x] = value
        return carry

    lax.fori_loop(0, bx, prepare, 0)
    clear(acc_f)
    spread_take("u", 3, sent, 0)
    spread_take("u", 3, sent, 1)

    def bond(x, k, mine):
        ex, ey, ez = offsets[k]
        part = slice(PAD + ey, PAD + ey + by)
        other = [uz[ez + 3, x + ex, c, part, :] for c in range(3)]
        if ex:
            other[0] = other[0] + float(ex)
        if ey:
            other[1] = other[1] + float(ey)
        return [other[c] - mine[c] for c in range(3)], part

    def dilate(x, carry):
        mine = [u[x, c, own, :] for c in range(3)]
        total = jnp.zeros((by, bz), jnp.float32)
        for k in ORDER:
            ex, ey, ez = offsets[k]
            d, part = bond(x, k, mine)
            radius = math.sqrt(square(offsets[k]))
            weight = math.exp(-square(offsets[k]) / 9.0)
            long2 = d[0] * d[0] + d[1] * d[1] + d[2] * d[2]
            ext = long2 * lax.rsqrt(long2) - radius
            term = jf[k, x] * (3.0 / volume * weight * radius) * ext
            ext_s[k, x] = ext
            len_s[k, x] = long2
            total = total + term
            acc_t[ez + 3, x + ex, 0, part, :] += term
        acc_t[3, x, 0, own, :] += total
        return carry

    def sweep(work, name, comps):
        lax.fori_loop(0, 3, lambda i, carry: work(bx - 1 - i, carry), 0)
        sent = fold_send(name, comps, 1)
        lax.fori_loop(0, bx - 3, lambda i, carry: work(bx - 4 - i, carry), 0)
        return sent + fold_send(name, comps, 0)

    def soften(part):
        def body(x, carry):
            for k in part:
                radius = math.sqrt(square(offsets[k]))
                weight = math.exp(-square(offsets[k]) / 9.0)
                ext = ext_s[k, x]
                more = 1.0 + (ext * ext) * (1.0 / (radius * soft_stretch) ** 2)
                scale = jf[k, x] * lax.rsqrt(more * more * len_s[k, x])
                a = 3.0 * bulk_modulus / volume * weight * radius
                b = 15.0 * shear_modulus / volume * weight
                len_s[k, x] = scale * (a - b * radius / 3.0)
                ext_s[k, x] = scale * ext * (2.0 * b)
            return carry

        lax.fori_loop(0, bx, body, 0)

    cut = (2 * len(ORDER)) // 3
    sent = sweep(dilate, "t", 1)
    soften(ORDER[:cut])

    def write_theta(x, c, value):
        theta_out[x] = value
        B["t_own"][0, x] = value
        t[x, 0, own, :] = value

    fold_take("t", 1, sent, write_theta)
    mx, whole = spread("t", 1, B["t_own"].at[:, 0:3])
    sent = spread_send("t", mx, whole)
    soften(ORDER[cut:])
    spread_take("t", 1, sent, 0)
    spread_take("t", 1, sent, 1)

    def push(x, carry):
        mine = [u[x, c, own, :] for c in range(3)]
        here = t[x, 0, own, :]
        total = [jnp.zeros((by, bz), jnp.float32) for c in range(3)]
        for k in ORDER:
            ex, ey, ez = offsets[k]
            d, part = bond(x, k, mine)
            scalar = len_s[k, x] * (here + tz[ez + 3, x + ex, 0, part, :]) + ext_s[k, x]
            for c in range(3):
                pushed = scalar * d[c]
                total[c] = total[c] + pushed
                acc_f[ez + 3, x + ex, c, part, :] -= pushed
        for c in range(3):
            acc_f[3, x, c, own, :] += total[c]
        return carry

    sent = sweep(push, "u", 3)

    def write_force(x, c, value):
        force_out[c, x] = value

    fold_take("u", 3, sent, write_force)
    for copy in copies:
        copy.finish()


def shards(sizes, displacement, bond_intact):
    plan = scratch_plan(bond_intact.shape[0], *displacement.shape[1:])
    plan["t_own"] = (1,) + displacement.shape[1:]
    scratch = [pltpu.VMEM(shape, jnp.float32) for shape in plan.values()]
    scratch += [
        pltpu.VMEM(bond_intact.shape, jnp.int32),
        pltpu.SemaphoreType.DMA((68,)),
        pltpu.SemaphoreType.DMA((68,)),
        pltpu.SemaphoreType.DMA((2,)),
    ]
    vmem, anywhere = pl.BlockSpec(memory_space=pltpu.VMEM), pl.BlockSpec(memory_space=pl.ANY)
    return pl.pallas_call(
        functools.partial(kernel, sizes, tuple(plan)),
        out_shape=(
            jax.ShapeDtypeStruct(displacement.shape, jnp.float32),
            jax.ShapeDtypeStruct(displacement.shape[1:], jnp.float32),
        ),
        in_specs=[anywhere, anywhere],
        out_specs=(vmem, vmem),
        scratch_shapes=scratch,
        compiler_params=pltpu.CompilerParams(collective_id=0, has_side_effects=True, vmem_limit_bytes=56000000),
    )(displacement, bond_intact)


def solution(mesh):
    sizes = {a: mesh.shape[a] for a in ("gx", "gy", "gz")}
    return jax.shard_map(
        functools.partial(shards, sizes),
        mesh=mesh,
        in_specs=(P(None, "gx", "gy", "gz"), P(None, "gx", "gy", "gz")),
        out_specs=(P(None, "gx", "gy", "gz"), P("gx", "gy", "gz")),
        check_vma=False,
    )
```
